1024 devices in a mesh: cin: 16 (over x, core), cout: 64 (over z, y).
Axes of the slice: x: 8, y: 8, z: 8, core: 2. Of those that a mesh axis runs over, the one named last changes fastest.
Arguments:
- inputs: bfloat16 [4096, 4, 128], P(('cin', 'cout')), may hold values from -6 to 6
- cotangent: bfloat16 [4096, 4, 128], P(('cout', 'cin')), may hold values from -6 to 6
- matrices: bfloat16 [24, 4096, 4096], P(None, 'cout', 'cin'), may hold values from -0.09375 to 0.09375
- filters: float32 [24, 128], replicated, may hold values from -0.109375 to 0.109375
Outputs:
- matrix_grads: bfloat16 [24, 4096, 4096], P(None, 'cout', 'cin')
- input_grads: bfloat16 [4096, 4, 128], P(('cin', 'cout'))
The draws below stay inside these ranges and needn't reach their ends.
All inputs are finite; a program needn't handle non-finite values.
Results may differ from the reference program's by a relative error of at most 0.002.
Values may be sent and summed in bfloat16 or wider, within the bound.
A program may use at most 32 MiB of HBM per device.

```python
import jax
import jax.numpy as jnp
from jax import lax

D = 4096
K = 24
B = 4
L = 128


def level_of(stream_key, dims, shards, smallest, high):
    level = 1.0
    for position, parts in shards:
        heights = jax.random.uniform(jax.random.fold_in(jax.random.fold_in(stream_key, 6), position), (parts,), jnp.float32, smallest / len(shards), high / len(shards))
        level = level * jnp.repeat(jnp.exp(heights), dims[position] // parts).reshape((-1,) + (1,) * (len(dims) - 1 - position))
    return level


def normal_values(rng, extent, scale, limit, cuts=(), held_as=jnp.bfloat16):
    entries = scale * jax.random.normal(rng, extent, jnp.float32)
    if cuts:
        entries = entries * level_of(rng, extent, cuts, -0.22, 0.18)
    return jnp.clip(entries, -limit, limit).astype(held_as)


def setup_inputs(seed: int = 0) -> dict:
    keys = jax.random.split(jax.random.key(seed), 5)
    return {
        "inputs": normal_values(keys[0], (D, B, L), 1.0, 6.0, ((0, 1024),)),
        "cotangent": normal_values(keys[1], (D, B, L), 1.0, 6.0, ((0, 1024),)),
        "matrices": normal_values(keys[2], (K, D, D), D ** -0.5, 0.09375, ((1, 64), (2, 16))),
        "filters": normal_values(keys[3], (K, L), (K * L) ** -0.5, 0.109375, (), jnp.float32),
    }


def toeplitz_upper(filter_row):
    length = filter_row.shape[0]
    padded = jnp.concatenate([filter_row, jnp.zeros((length,), filter_row.dtype)])
    tiled_rows = jnp.tile(padded, length)[: length * (2 * length - 1)]
    return tiled_rows.reshape(length, 2 * length - 1)[:, :length]


def reference(inputs, cotangent, matrices, filters):
    highest = lax.Precision.HIGHEST
    width = inputs.shape[0]
    length = inputs.shape[2]
    inputs_wide = inputs.astype(jnp.float32).reshape(width, -1)
    grads_wide = cotangent.astype(jnp.float32).reshape(width, -1)

    def per_filter(pair):
        filter_row, matrix_tile = pair
        upper_table = toeplitz_upper(filter_row)
        filtered = jnp.dot(inputs_wide.reshape(-1, length), upper_table, precision=highest).reshape(width, -1)
        matrix_grad = jnp.dot(grads_wide, filtered.T, precision=highest).astype(jnp.bfloat16)
        backward = jnp.dot(matrix_tile.astype(jnp.float32).T, grads_wide, precision=highest)
        pulled = jnp.dot(backward.reshape(-1, length), upper_table.T, precision=highest)
        return matrix_grad, pulled.reshape(width, -1)

    matrix_grads, pulled_all = lax.map(per_filter, (filters, matrices))
    total = jnp.sum(pulled_all, axis=0).reshape(inputs.shape)
    return matrix_grads, total.astype(jnp.bfloat16)
```

```python
import functools

import jax
import jax.numpy as jnp
from jax import lax
from jax.experimental import pallas as pl
from jax.experimental.pallas import tpu as pltpu
from jax.sharding import PartitionSpec as P

MESH = pl.DeviceIdType.MESH
ROWS_Y = 8
NT = (((1,), (1,)), ((), ()))


def split(value):
    high = value.astype(jnp.bfloat16)
    return high, (value - high.astype(jnp.float32)).astype(jnp.bfloat16)


def selector(shape, source_of_row):
    row = lax.broadcasted_iota(jnp.int32, shape, 0)
    column = lax.broadcasted_iota(jnp.int32, shape, 1)
    return jnp.where(column == source_of_row(row), 1.0, 0.0).astype(jnp.bfloat16)


def product(left, right):
    return jnp.dot(left, right, preferred_element_type=jnp.float32)


def product_nt(left, right):
    return lax.dot_general(left, right, NT, preferred_element_type=jnp.float32)


def kernel(
    dims,
    x_ref, g_ref, m_ref, f_ref,
    mg_ref, ig_ref,
    g_all, x_all, m_all, f_all, toeplitz, m_turned, g_high, g_low, x_wide,
    part_a, part_b, land_a, land_b, mid_a, mid_b, last_a, last_b, final_rows,
    local_sem, g_send, g_recv, x_send, x_recv, x_send2, x_recv2,
    a_send, a_recv, b_send, b_recv, a_send2, a_recv2, b_send2, b_recv2,
):
    ncin, nz, ny, filters, out_width, in_width, seqs, length, shard = dims
    cin = lax.axis_index("cin")
    cout = lax.axis_index("cout")
    zi = cout // ny
    yi = cout % ny
    half = seqs // 2

    def to_cin(step):
        return {"cin": (cin + step) % ncin}

    def to_z(step):
        return {"cout": ((zi + step) % nz) * ny + yi}

    def to_y(step):
        return {"cout": zi * ny + (yi + step) % ny}

    def each(count, action):
        def one(step, carried):
            action(step)
            return carried
        lax.fori_loop(1, count, one, 0)

    def send(source, target, send_sem, recv_sem, device):
        pltpu.make_async_remote_copy(
            src_ref=source, dst_ref=target, send_sem=send_sem, recv_sem=recv_sem,
            device_id=device, device_id_type=MESH,
        ).start()

    def drain(ref, sem):
        pltpu.make_async_copy(ref, ref, sem).wait()

    load_m = pltpu.make_async_copy(m_ref, m_all, local_sem.at[0])
    load_f = pltpu.make_async_copy(f_ref, f_all, local_sem.at[1])
    load_f.start()
    load_m.start()
    pltpu.make_async_copy(g_ref, g_all.at[cin], g_recv).start()
    pltpu.make_async_copy(x_ref, x_all.at[cout], x_recv).start()

    barrier = pltpu.get_barrier_semaphore()
    each(ncin, lambda s: pl.semaphore_signal(barrier, inc=1, device_id=to_cin(s), device_id_type=MESH))
    each(ny, lambda s: pl.semaphore_signal(barrier, inc=1, device_id=to_y(s), device_id_type=MESH))
    each(nz, lambda s: pl.semaphore_signal(barrier, inc=1, device_id=to_z(s), device_id_type=MESH))
    pl.semaphore_wait(barrier, ncin + ny + nz - 3)

    each(ncin, lambda s: send(g_ref, g_all.at[cin], g_send, g_recv, to_cin(s)))
    each(ny, lambda s: send(x_ref, x_all.at[cout], x_send, x_recv, to_y(s)))

    load_f.wait()

    def make_table(k, carried):
        row = jnp.broadcast_to(f_all[pl.ds(k, 1), :], (length, length))
        turned = pltpu.roll(row, 0, 1, stride=1, stride_axis=0)
        s_index = lax.broadcasted_iota(jnp.int32, (length, length), 0)
        t_index = lax.broadcasted_iota(jnp.int32, (length, length), 1)
        high, low = split(jnp.where(t_index >= s_index, turned, 0.0))
        start = pl.multiple_of(k * length, length)
        toeplitz[pl.ds(start, length), 0:length] = high
        toeplitz[pl.ds(start, length), length:2 * length] = low
        return carried

    lax.fori_loop(0, filters, make_table, 0)

    own_row = x_all.at[pl.ds(pl.multiple_of(zi * ny, ny), ny)]
    drain(own_row, x_recv)
    each(nz, lambda s: send(own_row, own_row, x_send2, x_recv2, to_z(s)))

    load_m.wait()
    natural = selector((in_width, in_width), lambda r: r)
    swapped = selector(
        (in_width, in_width),
        lambda r: ((r // shard) % nz * ny + r // (shard * nz)) * shard + r % shard,
    )
    orders = jnp.concatenate([natural, swapped], axis=0)
    chunk = 4 * out_width

    def turn(j, carried):
        start = pl.multiple_of(j * chunk, chunk)
        m_turned[:, pl.ds(start, chunk)] = product_nt(
            orders, m_all[pl.ds(start, chunk), :]
        ).astype(jnp.bfloat16)
        return carried

    lax.fori_loop(0, filters * out_width // chunk, turn, 0)

    by_sequence = selector(
        (seqs * out_width, seqs * out_width),
        lambda r: r % out_width * seqs + r // out_width,
    )

    drain(g_all, g_recv)
    g_rows = product(by_sequence, g_all[...].reshape(seqs * out_width, length)).astype(jnp.bfloat16)
    g_twice = jnp.concatenate([g_rows, g_rows], axis=1)

    def pull(j, carried):
        table = toeplitz[pl.ds(pl.multiple_of(j * 2 * length, 2 * length), 2 * length), :]
        pulled = product_nt(g_twice, table)
        for side in range(2):
            start = pl.multiple_of((j * 2 + side) * out_width, out_width)
            for b in range(seqs):
                high, low = split(
                    pulled[b * out_width:(b + 1) * out_width, side * length:(side + 1) * length]
                )
                g_high[pl.ds(start, out_width), b * length:(b + 1) * length] = high
                g_low[pl.ds(start, out_width), b * length:(b + 1) * length] = low
        return carried

    lax.fori_loop(0, filters // 2, pull, 0)

    width = half * length
    rows_z = in_width // nz
    rows_y = in_width // ny
    part_a[...] = (
        product(m_turned[0:in_width, :], g_high[:, 0:width])
        + product(m_turned[0:in_width, :], g_low[:, 0:width])
    ).reshape(nz, rows_z, width)
    each(nz, lambda s: send(part_a.at[(zi + s) % nz], land_a.at[s - 1], a_send, a_recv, to_z(s)))
    part_b[...] = (
        product(m_turned[in_width:2 * in_width, :], g_high[:, width:2 * width])
        + product(m_turned[in_width:2 * in_width, :], g_low[:, width:2 * width])
    ).reshape(ny, rows_y, width)
    each(ny, lambda s: send(part_b.at[(yi + s) % ny], land_b.at[s - 1], b_send, b_recv, to_y(s)))

    drain(x_all.at[pl.ds(0, (nz - 1) * ny)], x_recv2)
    group = out_width
    per_group = group // shard
    for j in range(in_width // group):
        block = x_all[j * per_group:(j + 1) * per_group].reshape(seqs * group, length)
        sorted_rows = product(by_sequence, block).astype(jnp.bfloat16)
        for b in range(seqs):
            x_wide[j * group:(j + 1) * group, b * length:(b + 1) * length] = sorted_rows[
                b * group:(b + 1) * group, :
            ]

    def weigh(j, carried):
        rows = pl.ds(pl.multiple_of(j * chunk, chunk), chunk)
        mg_ref[rows, :] = (
            product_nt(g_high[rows, :], x_wide[...]) + product_nt(g_low[rows, :], x_wide[...])
        ).astype(jnp.bfloat16)
        return carried

    lax.fori_loop(0, filters * out_width // chunk, weigh, 0)

    drain(land_a, a_recv)
    sum_a = part_a[zi]
    for s in range(nz - 1):
        sum_a = sum_a + land_a[s]
    for j in range(ny):
        for b in range(half):
            mid_a[j, b * shard:(b + 1) * shard, :] = sum_a[
                j * shard:(j + 1) * shard, b * length:(b + 1) * length
            ]
    each(ny, lambda s: send(mid_a.at[(yi + s) % ny], last_a.at[s - 1], a_send2, a_recv2, to_y(s)))
    drain(land_b, b_recv)
    sum_b = part_b[yi]
    for s in range(ny - 1):
        sum_b = sum_b + land_b[s]
    for j in range(nz):
        for b in range(half):
            mid_b[j, b * shard:(b + 1) * shard, :] = sum_b[
                j * shard:(j + 1) * shard, b * length:(b + 1) * length
            ]
    each(nz, lambda s: send(mid_b.at[(zi + s) % nz], last_b.at[s - 1], b_send2, b_recv2, to_z(s)))

    drain(last_a, a_recv2)
    total_a = mid_a[yi]
    for s in range(ny - 1):
        total_a = total_a + last_a[s]
    drain(last_b, b_recv2)
    total_b = mid_b[zi]
    for s in range(nz - 1):
        total_b = total_b + last_b[s]
    for i in range(shard):
        for b in range(half):
            row = b * shard + i
            final_rows[i * seqs + b:i * seqs + b + 1, :] = total_a[row:row + 1, :]
            final_rows[i * seqs + half + b:i * seqs + half + b + 1, :] = total_b[row:row + 1, :]
    ig_ref[...] = final_rows[...].astype(jnp.bfloat16)

    drain(g_all.at[pl.ds(0, ncin - 1)], g_send)
    drain(x_all.at[pl.ds(0, ny - 1)], x_send)
    drain(x_all.at[pl.ds(0, (nz - 1) * ny)], x_send2)
    drain(land_a, a_send)
    drain(land_b, b_send)
    drain(last_a, a_send2)
    drain(last_b, b_send2)


def shards(ncin, ncout, inputs, cotangent, matrices, filter_rows):
    ny = ROWS_Y
    nz = ncout // ny
    shard, seqs, length = inputs.shape
    filters, out_width, in_width = matrices.shape
    width = seqs // 2 * length
    dims = (ncin, nz, ny, filters, out_width, in_width, seqs, length, shard)
    rows = filters * out_width
    bf16, f32 = jnp.bfloat16, jnp.float32
    dma = pltpu.SemaphoreType.DMA
    hbm = pl.BlockSpec(memory_space=pltpu.HBM)
    vmem = pl.BlockSpec(memory_space=pltpu.VMEM)
    matrix_grads, input_grads = pl.pallas_call(
        functools.partial(kernel, dims),
        out_shape=(
            jax.ShapeDtypeStruct((rows, in_width), bf16),
            jax.ShapeDtypeStruct((shard * seqs, length), bf16),
        ),
        in_specs=[hbm] * 4,
        out_specs=(vmem, vmem),
        scratch_shapes=[
            pltpu.VMEM((ncin, shard * seqs, length), bf16),
            pltpu.VMEM((ncout, shard * seqs, length), bf16),
            pltpu.VMEM((rows, in_width), bf16),
            pltpu.VMEM((filters, length), f32),
            pltpu.VMEM((filters * length, 2 * length), bf16),
            pltpu.VMEM((2 * in_width, rows), bf16),
            pltpu.VMEM((rows, seqs * length), bf16),
            pltpu.VMEM((rows, seqs * length), bf16),
            pltpu.VMEM((in_width, seqs * length), bf16),
            pltpu.VMEM((nz, in_width // nz, width), f32),
            pltpu.VMEM((ny, in_width // ny, width), f32),
            pltpu.VMEM((nz - 1, in_width // nz, width), f32),
            pltpu.VMEM((ny - 1, in_width // ny, width), f32),
            pltpu.VMEM((ny, seqs // 2 * shard, length), f32),
            pltpu.VMEM((nz, seqs // 2 * shard, length), f32),
            pltpu.VMEM((ny - 1, seqs // 2 * shard, length), f32),
            pltpu.VMEM((nz - 1, seqs // 2 * shard, length), f32),
            pltpu.VMEM((shard * seqs, length), f32),
            dma((2,)),
        ] + [dma] * 14,
        compiler_params=pltpu.CompilerParams(
            collective_id=0, has_side_effects=True, vmem_limit_bytes=40 * 1024 * 1024
        ),
    )(
        inputs.reshape(shard * seqs, length),
        cotangent.reshape(shard * seqs, length),
        matrices.reshape(rows, in_width),
        filter_rows,
    )
    return (
        matrix_grads.reshape(filters, out_width, in_width),
        input_grads.reshape(shard, seqs, length),
    )


def solution(mesh):
    placed = (
        P(("cin", "cout"), None, None),
        P(("cout", "cin"), None, None),
        P(None, "cout", "cin"),
        P(),
    )
    return jax.shard_map(
        functools.partial(shards, mesh.shape["cin"], mesh.shape["cout"]),
        mesh=mesh,
        in_specs=placed,
        out_specs=(P(None, "cout", "cin"), P(("cin", "cout"), None, None)),
        check_vma=False,
    )
```

```python
import functools

import jax
import jax.numpy as jnp
from jax import lax
from jax.experimental import pallas as pl
from jax.experimental.pallas import tpu as pltpu
from jax.sharding import PartitionSpec as P

MESH = pl.DeviceIdType.MESH
ROWS_Y = 8
NT = (((1,), (1,)), ((), ()))


def split(value):
    high = value.astype(jnp.bfloat16)
    return high, (value - high.astype(jnp.float32)).astype(jnp.bfloat16)


def selector(shape, source_of_row):
    row = lax.broadcasted_iota(jnp.int32, shape, 0)
    column = lax.broadcasted_iota(jnp.int32, shape, 1)
    return jnp.where(column == source_of_row(row), 1.0, 0.0).astype(jnp.bfloat16)


def product(left, right):
    return jnp.dot(left, right, preferred_element_type=jnp.float32)


def product_nt(left, right):
    return lax.dot_general(left, right, NT, preferred_element_type=jnp.float32)


def far_first(count):
    return sorted(range(1, count), key=lambda step: -min(step, count - step))


def kernel(
    dims,
    x_ref, g_ref, m_ref, f_ref,
    mg_ref, ig_ref,
    g_all, x_by_z, x_by_y, m_all, f_all, toeplitz, m_turned, g_high, g_low, x_wide,
    part_a, part_b, land_a, land_b, mid_a, mid_b, last_a, last_b, final_rows,
    load_sem, g_send, g_recv, g_send2, g_recv2, xz_send, xz_recv, xy_send, xy_recv,
    xz_send2, xz_recv2, xy_send2, xy_recv2,
    a_send, a_recv, b_send, b_recv, a_send2, a_recv2, b_send2, b_recv2,
):
    ncin, nz, ny, filters, out_width, in_width, seqs, length, shard = dims
    nx = ncin // 2
    cin = lax.axis_index("cin")
    cout = lax.axis_index("cout")
    xi = cin // 2
    core = cin % 2
    zi = cout // ny
    yi = cout % ny
    half = seqs // 2
    width = half * length
    piece = shard * seqs
    rows_z = in_width // nz
    rows_y = in_width // ny

    def to_x(step):
        return {"cin": (cin + 2 * step) % ncin}

    def to_z(step):
        return {"cout": (zi + step) % nz * ny + yi}

    def to_y(step):
        return {"cout": zi * ny + (yi + step) % ny}

    other_core = {"cin": cin + 1 - 2 * core}

    def send(source, target, send_sem, recv_sem, device):
        pltpu.make_async_remote_copy(
            src_ref=source, dst_ref=target, send_sem=send_sem, recv_sem=recv_sem,
            device_id=device, device_id_type=MESH,
        ).start()

    def drain(ref, sem):
        pltpu.make_async_copy(ref, ref, sem).wait()

    barrier = pltpu.get_barrier_semaphore()

    def signal(device):
        pl.semaphore_signal(barrier, inc=1, device_id=device, device_id_type=MESH)

    for s in far_first(nx):
        signal(to_x(s))
    for s in far_first(ny):
        signal(to_y(s))
    for s in far_first(nz):
        signal(to_z(s))
    signal(other_core)

    load_f = pltpu.make_async_copy(f_ref, f_all, load_sem.at[0])
    load_m = pltpu.make_async_copy(m_ref, m_all, load_sem.at[1])
    x_first, x_second = x_ref.at[pl.ds(0, piece // 2)], x_ref.at[pl.ds(piece // 2, piece // 2)]
    own_g, own_side = g_all.at[core, xi], g_all.at[core]
    own_z, row_z = x_by_z.at[zi, yi], x_by_z.at[zi]
    own_y, row_y = x_by_y.at[yi, zi], x_by_y.at[yi]
    load_f.start()
    pltpu.make_async_copy(g_ref, own_g, g_recv).start()
    pltpu.make_async_copy(x_first, own_z, xz_recv).start()
    pltpu.make_async_copy(x_second, own_y, xy_recv).start()
    load_m.start()

    def make_table(k, carried):
        row = jnp.broadcast_to(f_all[pl.ds(k, 1), :], (length, length))
        turned = pltpu.roll(row, 0, 1, stride=1, stride_axis=0)
        s_index = lax.broadcasted_iota(jnp.int32, (length, length), 0)
        t_index = lax.broadcasted_iota(jnp.int32, (length, length), 1)
        high, low = split(jnp.where(t_index >= s_index, turned, 0.0))
        start = pl.multiple_of(k * length, length)
        toeplitz[pl.ds(start, length), 0:length] = high
        toeplitz[pl.ds(start, length), length:2 * length] = low
        return carried

    pl.semaphore_wait(barrier, nx + ny + nz - 2)
    for s in far_first(nx):
        send(g_ref, own_g, g_send, g_recv, to_x(s))
    for s in far_first(ny):
        send(x_first, own_z, xz_send, xz_recv, to_y(s))
    for s in far_first(nz):
        send(x_second, own_y, xy_send, xy_recv, to_z(s))

    load_f.wait()
    lax.fori_loop(0, filters, make_table, 0, unroll=12 if filters % 12 == 0 else 1)

    load_m.wait()
    natural = selector((in_width, in_width), lambda r: r)
    swapped = selector(
        (in_width, in_width),
        lambda r: ((r // shard) % nz * ny + r // (shard * nz)) * shard + r % shard,
    )
    orders = jnp.concatenate([natural, swapped], axis=0)
    chunk = 4 * out_width
    chunks = filters * out_width // chunk

    def turn(j, carried):
        start = pl.multiple_of(j * chunk, chunk)
        m_turned[:, pl.ds(start, chunk)] = product_nt(
            orders, m_all[pl.ds(start, chunk), :]
        ).astype(jnp.bfloat16)
        return carried

    lax.fori_loop(0, chunks, turn, 0, unroll=chunks)

    by_sequence = selector(
        (seqs * out_width, seqs * out_width),
        lambda r: ((r // shard % 2) * nx + r % out_width // (2 * shard)) * piece
        + r % shard * seqs + r // out_width,
    )

    drain(own_side, g_recv)
    send(own_side, own_side, g_send2, g_recv2, other_core)
    drain(row_z, xz_recv)
    for s in far_first(nz):
        send(row_z, row_z, xz_send2, xz_recv2, to_z(s))
    drain(row_y, xy_recv)
    for s in far_first(ny):
        send(row_y, row_y, xy_send2, xy_recv2, to_y(s))

    drain(own_side, g_recv2)
    g_rows = product(by_sequence, g_all[...].reshape(seqs * out_width, length)).astype(jnp.bfloat16)
    g_twice = jnp.concatenate([g_rows, g_rows], axis=1)

    def pull(j, carried):
        table = toeplitz[pl.ds(pl.multiple_of(j * 2 * length, 2 * length), 2 * length), :]
        pulled = product_nt(g_twice, table)
        for side in range(2):
            start = pl.multiple_of((j * 2 + side) * out_width, out_width)
            for b in range(seqs):
                high, low = split(
                    pulled[b * out_width:(b + 1) * out_width, side * length:(side + 1) * length]
                )
                g_high[pl.ds(start, out_width), b * length:(b + 1) * length] = high
                g_low[pl.ds(start, out_width), b * length:(b + 1) * length] = low
        return carried

    lax.fori_loop(0, filters // 2, pull, 0, unroll=filters // 2)

    part_a[...] = (
        product(m_turned[0:in_width, :], g_high[:, 0:width])
        + product(m_turned[0:in_width, :], g_low[:, 0:width])
    ).reshape(nz, rows_z, width)
    for s in far_first(nz):
        send(part_a.at[(zi + s) % nz], land_a.at[s - 1], a_send, a_recv, to_z(s))
    part_b[...] = (
        product(m_turned[in_width:2 * in_width, :], g_high[:, width:2 * width])
        + product(m_turned[in_width:2 * in_width, :], g_low[:, width:2 * width])
    ).reshape(ny, rows_y, width)
    for s in far_first(ny):
        send(part_b.at[(yi + s) % ny], land_b.at[s - 1], b_send, b_recv, to_y(s))

    drain(x_by_z.at[pl.ds(0, nz - 1)], xz_recv2)
    drain(x_by_y.at[pl.ds(0, ny - 1)], xy_recv2)
    group = out_width
    planes = group // (ny * shard)
    pair = shard // 2

    def place(r):
        b, channel = r // group, r % group
        plane, y, i = channel // (ny * shard), channel // shard % ny, channel % shard
        by_z = (plane * ny + y) * pair + i % pair
        by_y = (y * planes + plane) * pair + i % pair
        return jnp.where(i < pair, by_z, planes * ny * pair + by_y) * seqs + b

    sorter = selector((seqs * group, seqs * group), place)
    for j in range(in_width // group):
        here = slice(j * planes, (j + 1) * planes)
        block = jnp.concatenate(
            [
                x_by_z[here].astype(jnp.float32).reshape(seqs * group // 2, length),
                x_by_y[:, here].astype(jnp.float32).reshape(seqs * group // 2, length),
            ],
            axis=0,
        ).astype(jnp.bfloat16)
        sorted_rows = product(sorter, block).astype(jnp.bfloat16)
        for b in range(seqs):
            x_wide[j * group:(j + 1) * group, b * length:(b + 1) * length] = sorted_rows[
                b * group:(b + 1) * group, :
            ]

    def weigh(j, carried):
        rows = pl.ds(pl.multiple_of(j * chunk, chunk), chunk)
        mg_ref[rows, :] = (
            product_nt(g_high[rows, :], x_wide[...]) + product_nt(g_low[rows, :], x_wide[...])
        ).astype(jnp.bfloat16)
        return carried

    lax.fori_loop(0, chunks, weigh, 0, unroll=chunks)

    def regroup(total, count, target):
        for j in range(count):
            for b in range(half):
                target[j, b * shard:(b + 1) * shard, :] = total[
                    j * shard:(j + 1) * shard, b * length:(b + 1) * length
                ]

    drain(land_a, a_recv)
    sum_a = part_a[zi]
    for s in range(nz - 1):
        sum_a = sum_a + land_a[s]
    regroup(sum_a, ny, mid_a)
    for s in far_first(ny):
        send(mid_a.at[(yi + s) % ny], last_a.at[s - 1], a_send2, a_recv2, to_y(s))
    drain(land_b, b_recv)
    sum_b = part_b[yi]
    for s in range(ny - 1):
        sum_b = sum_b + land_b[s]
    regroup(sum_b, nz, mid_b)
    for s in far_first(nz):
        send(mid_b.at[(zi + s) % nz], last_b.at[s - 1], b_send2, b_recv2, to_z(s))

    drain(last_a, a_recv2)
    total_a = mid_a[yi]
    for s in range(ny - 1):
        total_a = total_a + last_a[s]
    drain(last_b, b_recv2)
    total_b = mid_b[zi]
    for s in range(nz - 1):
        total_b = total_b + last_b[s]
    for i in range(shard):
        for b in range(half):
            row = b * shard + i
            final_rows[i * seqs + b:i * seqs + b + 1, :] = total_a[row:row + 1, :]
            final_rows[i * seqs + half + b:i * seqs + half + b + 1, :] = total_b[row:row + 1, :]
    ig_ref[...] = final_rows[...].astype(jnp.bfloat16)

    drain(g_all.at[0, pl.ds(0, nx - 1)], g_send)
    drain(own_side, g_send2)
    drain(x_by_z.at[0, pl.ds(0, ny - 1)], xz_send)
    drain(x_by_y.at[0, pl.ds(0, nz - 1)], xy_send)
    drain(x_by_z.at[pl.ds(0, nz - 1)], xz_send2)
    drain(x_by_y.at[pl.ds(0, ny - 1)], xy_send2)
    drain(land_a, a_send)
    drain(land_b, b_send)
    drain(last_a, a_send2)
    drain(last_b, b_send2)


def shards(ncin, ncout, inputs, cotangent, matrices, filter_rows):
    ny = ROWS_Y
    nz = ncout // ny
    shard, seqs, length = inputs.shape
    filters, out_width, in_width = matrices.shape
    width = seqs // 2 * length
    dims = (ncin, nz, ny, filters, out_width, in_width, seqs, length, shard)
    rows = filters * out_width
    bf16, f32 = jnp.bfloat16, jnp.float32
    dma = pltpu.SemaphoreType.DMA
    hbm = pl.BlockSpec(memory_space=pltpu.HBM)
    vmem = pl.BlockSpec(memory_space=pltpu.VMEM)
    pinned = [
        pltpu.with_memory_space_constraint(value, pltpu.HBM)
        for value in (
            inputs.reshape(shard * seqs, length),
            cotangent.reshape(shard * seqs, length),
            matrices.reshape(rows, in_width),
            filter_rows,
        )
    ]
    matrix_grads, input_grads = pl.pallas_call(
        functools.partial(kernel, dims),
        out_shape=(
            jax.ShapeDtypeStruct((rows, in_width), bf16),
            jax.ShapeDtypeStruct((shard * seqs, length), bf16),
        ),
        in_specs=[hbm] * 4,
        out_specs=(vmem, vmem),
        scratch_shapes=[
            pltpu.VMEM((2, ncin // 2, shard * seqs, length), bf16),
            pltpu.VMEM((nz, ny, shard * seqs // 2, length), bf16),
            pltpu.VMEM((ny, nz, shard * seqs // 2, length), bf16),
            pltpu.VMEM((rows, in_width), bf16),
            pltpu.VMEM((filters, length), f32),
            pltpu.VMEM((filters * length, 2 * length), bf16),
            pltpu.VMEM((2 * in_width, rows), bf16),
            pltpu.VMEM((rows, seqs * length), bf16),
            pltpu.VMEM((rows, seqs * length), bf16),
            pltpu.VMEM((in_width, seqs * length), bf16),
            pltpu.VMEM((nz, in_width // nz, width), f32),
            pltpu.VMEM((ny, in_width // ny, width), f32),
            pltpu.VMEM((nz - 1, in_width // nz, width), f32),
            pltpu.VMEM((ny - 1, in_width // ny, width), f32),
            pltpu.VMEM((ny, seqs // 2 * shard, length), f32),
            pltpu.VMEM((nz, seqs // 2 * shard, length), f32),
            pltpu.VMEM((ny - 1, seqs // 2 * shard, length), f32),
            pltpu.VMEM((nz - 1, seqs // 2 * shard, length), f32),
            pltpu.VMEM((shard * seqs, length), f32),
            dma((2,)),
        ] + [dma] * 20,
        compiler_params=pltpu.CompilerParams(
            collective_id=0, has_side_effects=True, vmem_limit_bytes=40 * 1024 * 1024
        ),
    )(*pinned)
    return (
        matrix_grads.reshape(filters, out_width, in_width),
        input_grads.reshape(shard, seqs, length),
    )


def solution(mesh):
    placed = (
        P(("cin", "cout"), None, None),
        P(("cout", "cin"), None, None),
        P(None, "cout", "cin"),
        P(),
    )
    return jax.shard_map(
        functools.partial(shards, mesh.shape["cin"], mesh.shape["cout"]),
        mesh=mesh,
        in_specs=placed,
        out_specs=(P(None, "cout", "cin"), P(("cin", "cout"), None, None)),
        check_vma=False,
    )
```

```python
import functools

import jax
import jax.numpy as jnp
from jax import lax
from jax.experimental import pallas as pl
from jax.experimental.pallas import tpu as pltpu
from jax.sharding import PartitionSpec as P

MESH = pl.DeviceIdType.MESH
ROWS_Y = 8
NT = (((1,), (1,)), ((), ()))


def split(value):
    high = value.astype(jnp.bfloat16)
    return high, (value - high.astype(jnp.float32)).astype(jnp.bfloat16)


def selector(shape, source_of_row):
    row = lax.broadcasted_iota(jnp.int32, shape, 0)
    column = lax.broadcasted_iota(jnp.int32, shape, 1)
    return jnp.where(column == source_of_row(row), 1.0, 0.0).astype(jnp.bfloat16)


def product(left, right):
    return jnp.dot(left, right, preferred_element_type=jnp.float32)


def product_nt(left, right):
    return lax.dot_general(left, right, NT, preferred_element_type=jnp.float32)


def far_first(count):
    return sorted(range(1, count), key=lambda step: -min(step, count - step))


def kernel(
    dims,
    x_ref, g_ref, m_ref, f_ref,
    mg_ref, ig_ref,
    g_all, x_all, m_all, f_all, toeplitz, m_turned, g_high, g_low, x_wide,
    part_a, part_b, land_a, land_b, mid_a, mid_b, last_a, last_b, final_rows,
    ready, load_sem, g_send, g_recv, g_send2, g_recv2, x_send, x_recv, x_send2, x_recv2,
    a_send, a_recv, b_send, b_recv, a_send2, a_recv2, b_send2, b_recv2,
):
    ncin, nz, ny, filters, out_width, in_width, seqs, length, shard = dims
    nx = ncin // 2
    cin = lax.axis_index("cin")
    cout = lax.axis_index("cout")
    xi = cin // 2
    core = cin % 2
    zi = cout // ny
    yi = cout % ny
    half = seqs // 2
    width = half * length
    piece = shard * seqs
    rows_z = in_width // nz
    rows_y = in_width // ny

    def to_x(step):
        return {"cin": (cin + 2 * step) % ncin}

    def to_z(step):
        return {"cout": (zi + step) % nz * ny + yi}

    def to_y(step):
        return {"cout": zi * ny + (yi + step) % ny}

    other_core = {"cin": cin + 1 - 2 * core}

    def send(source, target, send_sem, recv_sem, device):
        pltpu.make_async_remote_copy(
            src_ref=source, dst_ref=target, send_sem=send_sem, recv_sem=recv_sem,
            device_id=device, device_id_type=MESH,
        ).start()

    def drain(ref, sem):
        pltpu.make_async_copy(ref, ref, sem).wait()

    barrier = pltpu.get_barrier_semaphore()

    def signal(sem, device):
        pl.semaphore_signal(sem, inc=1, device_id=device, device_id_type=MESH)

    signal(barrier, other_core)
    for s in far_first(nx):
        signal(barrier, {"cin": 2 * ((xi + s) % nx)})
    for s in far_first(ny):
        signal(barrier, {"cin": 2 * xi + 1, **to_y(s)})
    for s in far_first(nz):
        signal(barrier, {"cin": 2 * xi + 1, **to_z(s)})

    load_f = pltpu.make_async_copy(f_ref, f_all, load_sem.at[0])
    load_m = pltpu.make_async_copy(m_ref, m_all, load_sem.at[1])
    own_g, own_side = g_all.at[core, xi], g_all.at[core]
    own_x, row_x = x_all.at[yi, zi], x_all.at[yi]
    load_f.start()
    pltpu.make_async_copy(g_ref, own_g, g_recv).start()
    pltpu.make_async_copy(x_ref, own_x, x_recv).start()
    load_m.start()

    def make_table(k, carried):
        row = jnp.broadcast_to(f_all[pl.ds(k, 1), :], (length, length))
        turned = pltpu.roll(row, 0, 1, stride=1, stride_axis=0)
        s_index = lax.broadcasted_iota(jnp.int32, (length, length), 0)
        t_index = lax.broadcasted_iota(jnp.int32, (length, length), 1)
        high, low = split(jnp.where(t_index >= s_index, turned, 0.0))
        start = pl.multiple_of(k * length, length)
        toeplitz[pl.ds(start, length), 0:length] = high
        toeplitz[pl.ds(start, length), length:2 * length] = low
        return carried

    @pl.when(core == 0)
    def _():
        pl.semaphore_wait(barrier, 2 * (nx - 1) + 1)
        signal(ready, other_core)

    @pl.when(core == 1)
    def _():
        pl.semaphore_wait(ready, 1)

    for s in far_first(nx):
        send(g_ref, own_g, g_send, g_recv, to_x(s))

    load_f.wait()
    lax.fori_loop(0, filters, make_table, 0, unroll=12 if filters % 12 == 0 else 1)

    load_m.wait()
    natural = selector((in_width, in_width), lambda r: r)
    swapped = selector(
        (in_width, in_width),
        lambda r: ((r // shard) % nz * ny + r // (shard * nz)) * shard + r % shard,
    )
    orders = jnp.concatenate([natural, swapped], axis=0)
    chunk = 4 * out_width
    chunks = filters * out_width // chunk

    def turn(j, carried):
        start = pl.multiple_of(j * chunk, chunk)
        m_turned[:, pl.ds(start, chunk)] = product_nt(
            orders, m_all[pl.ds(start, chunk), :]
        ).astype(jnp.bfloat16)
        return carried

    lax.fori_loop(0, chunks, turn, 0, unroll=chunks)

    @pl.when(core == 1)
    def _():
        pl.semaphore_wait(barrier, 2 * (ny + nz - 2) + 1)
        signal(ready, other_core)

    @pl.when(core == 0)
    def _():
        pl.semaphore_wait(ready, 1)

    for s in far_first(nz):
        send(x_ref, own_x, x_send, x_recv, to_z(s))

    by_sequence = selector(
        (seqs * out_width, seqs * out_width),
        lambda r: ((r // shard % 2) * nx + r % out_width // (2 * shard)) * piece
        + r % shard * seqs + r // out_width,
    )

    drain(own_side, g_recv)
    send(own_side, own_side, g_send2, g_recv2, other_core)

    drain(own_side, g_recv2)
    g_rows = product(by_sequence, g_all[...].reshape(seqs * out_width, length)).astype(jnp.bfloat16)
    g_twice = jnp.concatenate([g_rows, g_rows], axis=1)

    def pull(j, carried):
        table = toeplitz[pl.ds(pl.multiple_of(j * 2 * length, 2 * length), 2 * length), :]
        pulled = product_nt(g_twice, table)
        for side in range(2):
            start = pl.multiple_of((j * 2 + side) * out_width, out_width)
            for b in range(seqs):
                high, low = split(
                    pulled[b * out_width:(b + 1) * out_width, side * length:(side + 1) * length]
                )
                g_high[pl.ds(start, out_width), b * length:(b + 1) * length] = high
                g_low[pl.ds(start, out_width), b * length:(b + 1) * length] = low
        return carried

    lax.fori_loop(0, filters // 2, pull, 0, unroll=filters // 2)

    part_b[...] = (
        product(m_turned[in_width:2 * in_width, :], g_high[:, width:2 * width])
        + product(m_turned[in_width:2 * in_width, :], g_low[:, width:2 * width])
    ).reshape(ny, rows_y, width)
    for s in far_first(ny):
        send(part_b.at[(yi + s) % ny], land_b.at[s - 1], b_send, b_recv, to_y(s))
    part_a[...] = (
        product(m_turned[0:in_width, :], g_high[:, 0:width])
        + product(m_turned[0:in_width, :], g_low[:, 0:width])
    ).reshape(nz, rows_z, width)
    for s in far_first(nz):
        send(part_a.at[(zi + s) % nz], land_a.at[s - 1], a_send, a_recv, to_z(s))

    drain(row_x, x_recv)
    for s in far_first(ny):
        send(row_x, row_x, x_send2, x_recv2, to_y(s))

    def regroup(total, count, target):
        for j in range(count):
            for b in range(half):
                target[j, b * shard:(b + 1) * shard, :] = total[
                    j * shard:(j + 1) * shard, b * length:(b + 1) * length
                ]

    drain(land_a, a_recv)
    sum_a = part_a[zi]
    for s in range(nz - 1):
        sum_a = sum_a + land_a[s]
    regroup(sum_a, ny, mid_a)
    for s in far_first(ny):
        send(mid_a.at[(yi + s) % ny], last_a.at[s - 1], a_send2, a_recv2, to_y(s))
    drain(land_b, b_recv)
    sum_b = part_b[yi]
    for s in range(ny - 1):
        sum_b = sum_b + land_b[s]
    regroup(sum_b, nz, mid_b)
    for s in far_first(nz):
        send(mid_b.at[(zi + s) % nz], last_b.at[s - 1], b_send2, b_recv2, to_z(s))

    drain(x_all.at[pl.ds(0, ny - 1)], x_recv2)
    group = out_width
    planes = group // (ny * shard)

    def place(r):
        b, channel = r // group, r % group
        plane, y, i = channel // (ny * shard), channel // shard % ny, channel % shard
        return ((y * planes + plane) * shard + i) * seqs + b

    sorter = selector((seqs * group, seqs * group), place)
    for j in range(in_width // group):
        block = x_all[:, j * planes:(j + 1) * planes].reshape(seqs * group, length)
        sorted_rows = product(sorter, block).astype(jnp.bfloat16)
        for b in range(seqs):
            x_wide[j * group:(j + 1) * group, b * length:(b + 1) * length] = sorted_rows[
                b * group:(b + 1) * group, :
            ]

    def weigh(j, carried):
        rows = pl.ds(pl.multiple_of(j * chunk, chunk), chunk)
        mg_ref[rows, :] = (
            product_nt(g_high[rows, :], x_wide[...]) + product_nt(g_low[rows, :], x_wide[...])
        ).astype(jnp.bfloat16)
        return carried

    lax.fori_loop(0, chunks, weigh, 0, unroll=chunks)

    drain(last_a, a_recv2)
    total_a = mid_a[yi]
    for s in range(ny - 1):
        total_a = total_a + last_a[s]
    drain(last_b, b_recv2)
    total_b = mid_b[zi]
    for s in range(nz - 1):
        total_b = total_b + last_b[s]
    for i in range(shard):
        for b in range(half):
            row = b * shard + i
            final_rows[i * seqs + b:i * seqs + b + 1, :] = total_a[row:row + 1, :]
            final_rows[i * seqs + half + b:i * seqs + half + b + 1, :] = total_b[row:row + 1, :]
    ig_ref[...] = final_rows[...].astype(jnp.bfloat16)

    drain(g_all.at[0, pl.ds(0, nx - 1)], g_send)
    drain(own_side, g_send2)
    drain(x_all.at[0, pl.ds(0, nz - 1)], x_send)
    drain(x_all.at[pl.ds(0, ny - 1)], x_send2)
    drain(land_a, a_send)
    drain(land_b, b_send)
    drain(last_a, a_send2)
    drain(last_b, b_send2)


def shards(ncin, ncout, inputs, cotangent, matrices, filter_rows):
    ny = ROWS_Y
    nz = ncout // ny
    shard, seqs, length = inputs.shape
    filters, out_width, in_width = matrices.shape
    width = seqs // 2 * length
    dims = (ncin, nz, ny, filters, out_width, in_width, seqs, length, shard)
    rows = filters * out_width
    bf16, f32 = jnp.bfloat16, jnp.float32
    dma = pltpu.SemaphoreType.DMA
    hbm = pl.BlockSpec(memory_space=pltpu.HBM)
    vmem = pl.BlockSpec(memory_space=pltpu.VMEM)
    pinned = [
        pltpu.with_memory_space_constraint(value, pltpu.HBM)
        for value in (
            inputs.reshape(shard * seqs, length),
            cotangent.reshape(shard * seqs, length),
            matrices.reshape(rows, in_width),
            filter_rows,
        )
    ]
    matrix_grads, input_grads = pl.pallas_call(
        functools.partial(kernel, dims),
        out_shape=(
            jax.ShapeDtypeStruct((rows, in_width), bf16),
            jax.ShapeDtypeStruct((shard * seqs, length), bf16),
        ),
        in_specs=[hbm] * 4,
        out_specs=(vmem, vmem),
        scratch_shapes=[
            pltpu.VMEM((2, ncin // 2, shard * seqs, length), bf16),
            pltpu.VMEM((ny, nz, shard * seqs, length), bf16),
            pltpu.VMEM((rows, in_width), bf16),
            pltpu.VMEM((filters, length), f32),
            pltpu.VMEM((filters * length, 2 * length), bf16),
            pltpu.VMEM((2 * in_width, rows), bf16),
            pltpu.VMEM((rows, seqs * length), bf16),
            pltpu.VMEM((rows, seqs * length), bf16),
            pltpu.VMEM((in_width, seqs * length), bf16),
            pltpu.VMEM((nz, in_width // nz, width), f32),
            pltpu.VMEM((ny, in_width // ny, width), f32),
            pltpu.VMEM((nz - 1, in_width // nz, width), f32),
            pltpu.VMEM((ny - 1, in_width // ny, width), f32),
            pltpu.VMEM((ny, seqs // 2 * shard, length), f32),
            pltpu.VMEM((nz, seqs // 2 * shard, length), f32),
            pltpu.VMEM((ny - 1, seqs // 2 * shard, length), f32),
            pltpu.VMEM((nz - 1, seqs // 2 * shard, length), f32),
            pltpu.VMEM((shard * seqs, length), f32),
            pltpu.SemaphoreType.REGULAR,
            dma((2,)),
        ] + [dma] * 16,
        compiler_params=pltpu.CompilerParams(
            collective_id=0, has_side_effects=True, vmem_limit_bytes=40 * 1024 * 1024
        ),
    )(*pinned)
    return (
        matrix_grads.reshape(filters, out_width, in_width),
        input_grads.reshape(shard, seqs, length),
    )


def solution(mesh):
    placed = (
        P(("cin", "cout"), None, None),
        P(("cout", "cin"), None, None),
        P(None, "cout", "cin"),
        P(),
    )
    return jax.shard_map(
        functools.partial(shards, mesh.shape["cin"], mesh.shape["cout"]),
        mesh=mesh,
        in_specs=placed,
        out_specs=(P(None, "cout", "cin"), P(("cin", "cout"), None, None)),
        check_vma=False,
    )
```

```python
import functools

import jax
import jax.numpy as jnp
from jax import lax
from jax.experimental import pallas as pl
from jax.experimental.pallas import tpu as pltpu
from jax.sharding import PartitionSpec as P

MESH = pl.DeviceIdType.MESH
ROWS_Y = 8
NT = (((1,), (1,)), ((), ()))


def split(value):
    high = value.astype(jnp.bfloat16)
    return high, (value - high.astype(jnp.float32)).astype(jnp.bfloat16)


def selector(shape, source_of_row):
    row = lax.broadcasted_iota(jnp.int32, shape, 0)
    column = lax.broadcasted_iota(jnp.int32, shape, 1)
    return jnp.where(column == source_of_row(row), 1.0, 0.0).astype(jnp.bfloat16)


def product(left, right):
    return jnp.dot(left, right, preferred_element_type=jnp.float32)


def product_nt(left, right):
    return lax.dot_general(left, right, NT, preferred_element_type=jnp.float32)


def far_first(count):
    return sorted(range(1, count), key=lambda step: -min(step, count - step))


def kernel(
    dims,
    x_ref, g_ref, m_ref, f_ref,
    mg_ref, ig_ref,
    g_all, x_all, m_all, f_all, toeplitz, m_turned, g_high, g_low, x_wide,
    part_a, part_b, land_a, land_b, mid_a, mid_b, last_a, last_b, final_rows,
    ready, load_sem, g_send, g_recv, g_send2, g_recv2, x_send, x_recv, x_send2, x_recv2,
    a_send, a_recv, b_send, b_recv, a_send2, a_recv2, b_send2, b_recv2,
):
    ncin, nz, ny, filters, out_width, in_width, seqs, length, shard = dims
    nx = ncin // 2
    cin = lax.axis_index("cin")
    cout = lax.axis_index("cout")
    xi = cin // 2
    core = cin % 2
    zi = cout // ny
    yi = cout % ny
    half = seqs // 2
    width = half * length
    piece = shard * seqs
    rows_z = in_width // nz
    rows_y = in_width // ny

    def to_x(step):
        return {"cin": (cin + 2 * step) % ncin}

    def to_z(step):
        return {"cout": (zi + step) % nz * ny + yi}

    def to_y(step):
        return {"cout": zi * ny + (yi + step) % ny}

    other_core = {"cin": cin + 1 - 2 * core}

    def send(source, target, send_sem, recv_sem, device):
        pltpu.make_async_remote_copy(
            src_ref=source, dst_ref=target, send_sem=send_sem, recv_sem=recv_sem,
            device_id=device, device_id_type=MESH,
        ).start()

    def drain(ref, sem):
        pltpu.make_async_copy(ref, ref, sem).wait()

    barrier = pltpu.get_barrier_semaphore()

    def signal(sem, device):
        pl.semaphore_signal(sem, inc=1, device_id=device, device_id_type=MESH)

    signal(barrier, other_core)
    for s in far_first(nx):
        signal(barrier, {"cin": 2 * ((xi + s) % nx)})
    for s in far_first(ny):
        signal(barrier, {"cin": 2 * xi + 1, **to_y(s)})
    for s in far_first(nz):
        signal(barrier, {"cin": 2 * xi + 1, **to_z(s)})

    load_f = pltpu.make_async_copy(f_ref, f_all, load_sem.at[0])
    load_m = pltpu.make_async_copy(m_ref, m_all, load_sem.at[1])
    own_g, own_side = g_all.at[core, xi], g_all.at[core]
    own_x, row_x = x_all.at[yi, zi], x_all.at[yi]
    load_f.start()
    pltpu.make_async_copy(g_ref, own_g, g_recv).start()
    pltpu.make_async_copy(x_ref, own_x, x_recv).start()
    load_m.start()

    def make_table(k, carried):
        row = jnp.broadcast_to(f_all[pl.ds(k, 1), :], (length, length))
        turned = pltpu.roll(row, 0, 1, stride=1, stride_axis=0)
        s_index = lax.broadcasted_iota(jnp.int32, (length, length), 0)
        t_index = lax.broadcasted_iota(jnp.int32, (length, length), 1)
        high, low = split(jnp.where(t_index >= s_index, turned, 0.0))
        start = pl.multiple_of(k * length, length)
        toeplitz[pl.ds(start, length), 0:length] = high
        toeplitz[pl.ds(start, length), length:2 * length] = low
        return carried

    @pl.when(core == 0)
    def _():
        pl.semaphore_wait(barrier, 2 * (nx - 1) + 1)
        signal(ready, other_core)

    @pl.when(core == 1)
    def _():
        pl.semaphore_wait(ready, 1)

    for s in far_first(nx):
        send(g_ref, own_g, g_send, g_recv, to_x(s))

    load_f.wait()
    lax.fori_loop(0, filters, make_table, 0, unroll=12 if filters % 12 == 0 else 1)

    load_m.wait()
    natural = selector((in_width, in_width), lambda r: r)
    swapped = selector(
        (in_width, in_width),
        lambda r: ((r // shard) % nz * ny + r // (shard * nz)) * shard + r % shard,
    )
    orders = jnp.concatenate([natural, swapped], axis=0)
    chunk = 4 * out_width
    chunks = filters * out_width // chunk

    def turn(j, carried):
        start = pl.multiple_of(j * chunk, chunk)
        m_turned[:, pl.ds(start, chunk)] = product_nt(
            orders, m_all[pl.ds(start, chunk), :]
        ).astype(jnp.bfloat16)
        return carried

    lax.fori_loop(0, chunks, turn, 0, unroll=chunks)

    @pl.when(core == 1)
    def _():
        pl.semaphore_wait(barrier, 2 * (ny + nz - 2) + 1)
        signal(ready, other_core)

    @pl.when(core == 0)
    def _():
        pl.semaphore_wait(ready, 1)

    for s in far_first(nz):
        send(x_ref, own_x, x_send, x_recv, to_z(s))

    by_sequence = selector(
        (seqs * out_width, seqs * out_width),
        lambda r: ((r // shard % 2) * nx + r % out_width // (2 * shard)) * piece
        + r % shard * seqs + r // out_width,
    )

    drain(own_side, g_recv)
    send(own_side, own_side, g_send2, g_recv2, other_core)

    drain(own_side, g_recv2)
    g_rows = product(by_sequence, g_all[...].reshape(seqs * out_width, length)).astype(jnp.bfloat16)
    g_twice = jnp.concatenate([g_rows, g_rows], axis=1)

    def pull(j, carried):
        table = toeplitz[pl.ds(pl.multiple_of(j * 2 * length, 2 * length), 2 * length), :]
        pulled = product_nt(g_twice, table)
        for side in range(2):
            start = pl.multiple_of((j * 2 + side) * out_width, out_width)
            for b in range(seqs):
                high, low = split(
                    pulled[b * out_width:(b + 1) * out_width, side * length:(side + 1) * length]
                )
                g_high[pl.ds(start, out_width), b * length:(b + 1) * length] = high
                g_low[pl.ds(start, out_width), b * length:(b + 1) * length] = low
        return carried

    lax.fori_loop(0, filters // 2, pull, 0, unroll=filters // 2)

    part_a[...] = (
        product(m_turned[0:in_width, :], g_high[:, 0:width])
        + product(m_turned[0:in_width, :], g_low[:, 0:width])
    ).reshape(nz, rows_z, width)
    for s in far_first(nz):
        send(part_a.at[(zi + s) % nz], land_a.at[s - 1], a_send, a_recv, to_z(s))
    part_b[...] = (
        product(m_turned[in_width:2 * in_width, :], g_high[:, width:2 * width])
        + product(m_turned[in_width:2 * in_width, :], g_low[:, width:2 * width])
    ).reshape(ny, rows_y, width)
    for s in far_first(ny):
        send(part_b.at[(yi + s) % ny], land_b.at[s - 1], b_send, b_recv, to_y(s))

    drain(row_x, x_recv)
    for s in far_first(ny):
        send(row_x, row_x, x_send2, x_recv2, to_y(s))

    def regroup(total, count, target):
        for j in range(count):
            for b in range(half):
                target[j, b * shard:(b + 1) * shard, :] = total[
                    j * shard:(j + 1) * shard, b * length:(b + 1) * length
                ]

    drain(land_a, a_recv)
    sum_a = part_a[zi]
    for s in range(nz - 1):
        sum_a = sum_a + land_a[s]
    regroup(sum_a, ny, mid_a)
    for s in far_first(ny):
        send(mid_a.at[(yi + s) % ny], last_a.at[s - 1], a_send2, a_recv2, to_y(s))
    drain(land_b, b_recv)
    sum_b = part_b[yi]
    for s in range(ny - 1):
        sum_b = sum_b + land_b[s]
    regroup(sum_b, nz, mid_b)
    for s in far_first(nz):
        send(mid_b.at[(zi + s) % nz], last_b.at[s - 1], b_send2, b_recv2, to_z(s))

    drain(x_all.at[pl.ds(0, ny - 1)], x_recv2)
    group = out_width
    planes = group // (ny * shard)

    def place(r):
        b, channel = r // group, r % group
        plane, y, i = channel // (ny * shard), channel // shard % ny, channel % shard
        return ((y * planes + plane) * shard + i) * seqs + b

    sorter = selector((seqs * group, seqs * group), place)
    for j in range(in_width // group):
        block = x_all[:, j * planes:(j + 1) * planes].reshape(seqs * group, length)
        sorted_rows = product(sorter, block).astype(jnp.bfloat16)
        for b in range(seqs):
            x_wide[j * group:(j + 1) * group, b * length:(b + 1) * length] = sorted_rows[
                b * group:(b + 1) * group, :
            ]

    def weigh(j, carried):
        rows = pl.ds(pl.multiple_of(j * chunk, chunk), chunk)
        mg_ref[rows, :] = (
            product_nt(g_high[rows, :], x_wide[...]) + product_nt(g_low[rows, :], x_wide[...])
        ).astype(jnp.bfloat16)
        return carried

    lax.fori_loop(0, chunks, weigh, 0, unroll=chunks)

    drain(last_a, a_recv2)
    total_a = mid_a[yi]
    for s in range(ny - 1):
        total_a = total_a + last_a[s]
    drain(last_b, b_recv2)
    total_b = mid_b[zi]
    for s in range(nz - 1):
        total_b = total_b + last_b[s]
    for i in range(shard):
        for b in range(half):
            row = b * shard + i
            final_rows[i * seqs + b:i * seqs + b + 1, :] = total_a[row:row + 1, :]
            final_rows[i * seqs + half + b:i * seqs + half + b + 1, :] = total_b[row:row + 1, :]
    ig_ref[...] = final_rows[...].astype(jnp.bfloat16)

    drain(g_all.at[0, pl.ds(0, nx - 1)], g_send)
    drain(own_side, g_send2)
    drain(x_all.at[0, pl.ds(0, nz - 1)], x_send)
    drain(x_all.at[pl.ds(0, ny - 1)], x_send2)
    drain(land_a, a_send)
    drain(land_b, b_send)
    drain(last_a, a_send2)
    drain(last_b, b_send2)


def shards(ncin, ncout, inputs, cotangent, matrices, filter_rows):
    ny = ROWS_Y
    nz = ncout // ny
    shard, seqs, length = inputs.shape
    filters, out_width, in_width = matrices.shape
    width = seqs // 2 * length
    dims = (ncin, nz, ny, filters, out_width, in_width, seqs, length, shard)
    rows = filters * out_width
    bf16, f32 = jnp.bfloat16, jnp.float32
    dma = pltpu.SemaphoreType.DMA
    hbm = pl.BlockSpec(memory_space=pltpu.HBM)
    vmem = pl.BlockSpec(memory_space=pltpu.VMEM)
    pinned = [
        pltpu.with_memory_space_constraint(value, pltpu.HBM)
        for value in (
            inputs.reshape(shard * seqs, length),
            cotangent.reshape(shard * seqs, length),
            matrices.reshape(rows, in_width),
            filter_rows,
        )
    ]
    matrix_grads, input_grads = pl.pallas_call(
        functools.partial(kernel, dims),
        out_shape=(
            jax.ShapeDtypeStruct((rows, in_width), bf16),
            jax.ShapeDtypeStruct((shard * seqs, length), bf16),
        ),
        in_specs=[hbm] * 4,
        out_specs=(vmem, vmem),
        scratch_shapes=[
            pltpu.VMEM((2, ncin // 2, shard * seqs, length), bf16),
            pltpu.VMEM((ny, nz, shard * seqs, length), bf16),
            pltpu.VMEM((rows, in_width), bf16),
            pltpu.VMEM((filters, length), f32),
            pltpu.VMEM((filters * length, 2 * length), bf16),
            pltpu.VMEM((2 * in_width, rows), bf16),
            pltpu.VMEM((rows, seqs * length), bf16),
            pltpu.VMEM((rows, seqs * length), bf16),
            pltpu.VMEM((in_width, seqs * length), bf16),
            pltpu.VMEM((nz, in_width // nz, width), f32),
            pltpu.VMEM((ny, in_width // ny, width), f32),
            pltpu.VMEM((nz - 1, in_width // nz, width), f32),
            pltpu.VMEM((ny - 1, in_width // ny, width), f32),
            pltpu.VMEM((ny, seqs // 2 * shard, length), f32),
            pltpu.VMEM((nz, seqs // 2 * shard, length), f32),
            pltpu.VMEM((ny - 1, seqs // 2 * shard, length), f32),
            pltpu.VMEM((nz - 1, seqs // 2 * shard, length), f32),
            pltpu.VMEM((shard * seqs, length), f32),
            pltpu.SemaphoreType.REGULAR,
            dma((2,)),
        ] + [dma] * 16,
        compiler_params=pltpu.CompilerParams(
            collective_id=0, has_side_effects=True, vmem_limit_bytes=40 * 1024 * 1024
        ),
    )(*pinned)
    return (
        matrix_grads.reshape(filters, out_width, in_width),
        input_grads.reshape(shard, seqs, length),
    )


def solution(mesh):
    placed = (
        P(("cin", "cout"), None, None),
        P(("cout", "cin"), None, None),
        P(None, "cout", "cin"),
        P(),
    )
    return jax.shard_map(
        functools.partial(shards, mesh.shape["cin"], mesh.shape["cout"]),
        mesh=mesh,
        in_specs=placed,
        out_specs=(P(None, "cout", "cin"), P(("cin", "cout"), None, None)),
        check_vma=False,
    )
```
